32 devices in a mesh: dp: 2 (over x), expert: 16 (over z, y, core).
Axes of the slice: x: 2, y: 2, z: 4, core: 2. Of those that a mesh axis runs over, the one named last changes fastest.
Arguments:
- q_latent: bfloat16 [128, 16, 576], P(('expert', 'dp')), may hold values from -48 to 48
- latent_cache: bfloat16 [128, 512, 576], P(('expert', 'dp')), may hold values from -10 to 10
- lengths: int32 [128], P(('expert', 'dp')), may hold values from 2 to 512
- residual: bfloat16 [128, 2048], P(('expert', 'dp')), may hold values from -6 to 6
- adapter_ids: int32 [128], P(('expert', 'dp')), may hold values from 0 to 31
- value_out: bfloat16 [8192, 2048], P('expert'), may hold values from -0.0625 to 0.0625
- adapter_down: bfloat16 [8192, 512], P('expert'), may hold values from -0.0625 to 0.0625
- adapter_up_factors: bfloat16 [512, 2048], P('expert'), may hold values from -1.5 to 1.5
- norm_gain: bfloat16 [2048], replicated, may hold values from 0.099609375 to 1.8984375
- expert_ids: int32 [128, 6], P('expert'), may hold values from 0 to 15, all different within a row; in each aligned block of 8 rows (0 to 7, 8 to 15, ...) at most 6 rows name the same one
- gate_weights: float32 [128, 6], P('expert'), may hold values from 0.05 to 0.5
- w_gate: bfloat16 [16, 2048, 1024], P('expert', None, 'dp'), may hold values from -0.125 to 0.125
- w_up: bfloat16 [16, 2048, 1024], P('expert', None, 'dp'), may hold values from -0.125 to 0.125
- w_down: bfloat16 [16, 2048, 1024], P('expert', None, 'dp'), may hold values from -0.1875 to 0.1875
Outputs:
- layer_out: bfloat16 [128, 2048], P(('expert', 'dp'))
The draws below stay inside these ranges and needn't reach their ends.
Inputs may be any that keep to these rules, and one draw needn't show every extreme that they name: `expert_ids`: each row names 6 different experts. Requests e * 8 to e * 8 + 7 form aligned blocks; in each block no expert is named by more than 6 rows, and in some block an expert is named by exactly 6 rows.
All inputs are finite; a program needn't handle non-finite values.
Results may differ from the reference program's by a relative error of at most 0.008.
Values may be sent and summed in bfloat16 or wider, within the bound.
A program may use at most 64 MiB of HBM per device.

```python
import math
import jax
import jax.numpy as jnp
import numpy as np
from jax import lax

D = 2048
HEADS = 16
LAT = 512
ROPE = 64
TOPK = 6
HID = 1024
ADAPTER_RANK = 16
CTX = 512
EXPERTS = 16
ADAPTER_TOTAL = 32
REQUEST_TOTAL = 128
COLUMN = 8
MOST = 6
N_EXPERT = 16


def draw_q_latent(key, part):
    shape = (REQUEST_TOTAL, HEADS, LAT + ROPE)
    query = jnp.clip(jax.random.normal(jax.random.fold_in(key, 5), shape, jnp.float32), -5.0, 5.0)
    return query.astype(jnp.bfloat16)


def draw_latent_cache(key, part):
    shape = (REQUEST_TOTAL, CTX, LAT + ROPE)
    cache_rows = jnp.clip(jax.random.normal(jax.random.fold_in(key, 8), shape, jnp.float32), -5.0, 5.0)
    return cache_rows.astype(jnp.bfloat16)


def place_ends(result, own_key, smallest, largest):
    index_at = [jax.random.randint(jax.random.fold_in(own_key, axis), (), 0, length) for axis, length in enumerate(result.shape)]
    longest = result.shape.index(max(result.shape))
    neighbour = index_at[:longest] + [(index_at[longest] + 1) % result.shape[longest]] + index_at[longest + 1:]
    return result.at[tuple(index_at)].set(smallest).at[tuple(neighbour)].set(largest)


def levels(stream_key, dims, shards, low, top_value):
    gain, own = 1.0, jax.random.fold_in(stream_key, 6)
    for position, parts in shards:
        draws = jnp.exp(jax.random.uniform(jax.random.fold_in(own, position), (parts,), jnp.float32, low / len(shards), top_value / len(shards)))
        gain = gain * jnp.repeat(draws, dims[position] // parts).reshape([-1 if axis == position else 1 for axis in range(len(dims))])
    return gain


def rank_bounds(count, slope):
    loads = [(1 << 20) // math.isqrt(standing ** slope) + 1 for standing in range(1, count + 1)]
    spread = 1 + sum(loads) // (1 << 30)
    return np.cumsum(np.array([max(1, weight // spread) for weight in loads]))


def skewed_ids(rng, extent, count, slope):
    table = rank_bounds(count, slope)
    lot = jax.random.randint(jax.random.fold_in(rng, 1), extent, 0, int(table[count - 1]))
    grade = jnp.searchsorted(jnp.asarray(table, jnp.int32), lot, side="right")
    return jax.random.permutation(jax.random.fold_in(rng, 2), count)[grade].astype(jnp.int32)


def deal_out(key, own, number, rows, count, top, most, skew):
    ranking = jax.random.permutation(key, count)
    crowded, usual = shares(count, rows * top, most, skew, True), shares(count, rows * top, most, skew, False)
    places = jnp.arange(count)

    def named(tallies, rotation):
        used = int((tallies > 0).sum())
        fixed = max(1, used // 4)
        passed = fixed + (places - fixed + rotation * (used - fixed)) % max(1, count - fixed)
        return jnp.zeros((count,), jnp.int32).at[ranking[jnp.where(places < fixed, places, passed)]].set(jnp.asarray(tallies, jnp.int32))

    tallies = jnp.where(number % 4 == 0, named(crowded, number // 4), named(usual, number - number // 4 - 1))
    mixed = jax.random.permutation(jax.random.fold_in(own, 3), count)
    giver, sink = mixed[0:count // 2 * 2:2], mixed[1:count // 2 * 2:2]
    slack = jnp.minimum(tallies[giver] - 1, most - tallies[sink]) // 2
    slack = jnp.where((giver == ranking[0]) | (sink == ranking[0]) | (tallies[sink] == 0), 0, jnp.maximum(slack, 0))
    passed = jax.random.randint(jax.random.fold_in(own, 4), (count // 2,), 0, 1 << 20) % (slack + 1)
    tallies = tallies.at[giver].add(-passed).at[sink].add(passed)
    items = jnp.searchsorted(jnp.cumsum(tallies), jnp.arange(rows * top), side="right").astype(jnp.int32)
    grid = items.reshape(top, rows).T
    grid = grid[jax.random.permutation(jax.random.fold_in(own, 1), rows)]
    rotation = jax.random.randint(jax.random.fold_in(own, 2), (rows, 1), 0, top)
    return jnp.take_along_axis(grid, (jnp.arange(top)[None, :] + rotation) % top, axis=1)


def shares(number_of, total, bound, skew, full):
    portions = [(1 << 20) // math.isqrt(standing ** skew) + 1 for standing in range(1, number_of + 1)]
    largest = bound if full else min(bound, max(-(-total // number_of), total * portions[0] // sum(portions)))
    least = 1 if total - largest >= number_of - 1 else 0
    holding, rest = [largest] + [least] * (number_of - 1), total - largest - least * (number_of - 1)
    while rest > 0:
        movable = [i for i in range(1, number_of) if holding[i] < largest] or [i for i in range(1, number_of) if holding[i] < bound]
        whole, left = sum([portions[i] for i in movable]), rest
        for i in movable:
            addition = min(bound - holding[i], max(1, left * portions[i] // whole), rest)
            holding[i] = holding[i] + addition
            rest = rest - addition
    return np.array(holding)


def scatter_about(key, dims, spread, reach, cuts=(), kind=jnp.bfloat16):
    drawn = jax.random.normal(key, dims, jnp.float32) * spread
    if len(cuts) > 0:
        drawn = levels(key, dims, cuts, -0.22, 0.18) * drawn
    return jnp.clip(drawn, min=-reach, max=reach).astype(kind)


def setup_inputs(seed: int = 0) -> dict:
    key_of = jax.random.split(jax.random.key(seed), 15)
    q_latent = draw_q_latent(jax.random.fold_in(key_of[14], 71), 0)
    latent_cache = draw_latent_cache(jax.random.fold_in(key_of[14], 71), 0)
    lengths = place_ends(jax.random.randint(key_of[2], (REQUEST_TOTAL,), 2, CTX + 1), jax.random.fold_in(key_of[2], 1), 2, CTX).astype(jnp.int32)
    residual = scatter_about(key_of[3], (REQUEST_TOTAL, D), 1.0, 6.0, ((0, 32),))
    adapter_ids = place_ends(skewed_ids(key_of[4], (REQUEST_TOTAL,), ADAPTER_TOTAL, 2), jax.random.fold_in(key_of[4], 3), 0, ADAPTER_TOTAL - 1).astype(jnp.int32)
    value_out = scatter_about(key_of[5], (HEADS * LAT, D), (HEADS * LAT) ** -0.5, 0.0625, ((0, 16),))
    adapter_down = scatter_about(key_of[6], (HEADS * LAT, ADAPTER_TOTAL * ADAPTER_RANK), (HEADS * LAT) ** -0.5, 0.0625, ((0, 16),))
    adapter_up_factors = scatter_about(key_of[7], (ADAPTER_TOTAL * ADAPTER_RANK, D), ADAPTER_RANK ** -0.5, 1.5, ((0, 16),))
    norm_gain = jnp.clip(1.0 + 0.18 * jax.random.normal(key_of[8], (D,), jnp.float32), 0.099609375, 1.8984375).astype(jnp.bfloat16)
    expert_ids_keys = jax.random.split(jax.random.fold_in(key_of[9], 1), REQUEST_TOTAL // COLUMN)
    expert_ids_turns = jax.random.permutation(jax.random.fold_in(key_of[9], 3), REQUEST_TOTAL // COLUMN)
    expert_ids = jax.vmap(lambda own, number: deal_out(jax.random.fold_in(key_of[9], 2), own, number, COLUMN, EXPERTS, TOPK, MOST, 2))(expert_ids_keys, expert_ids_turns).reshape((REQUEST_TOTAL, TOPK))
    gate_weights = jnp.clip(jnp.exp(math.log(0.5) - 2.3025851 * jax.random.uniform(key_of[10], (REQUEST_TOTAL, TOPK), jnp.float32) ** levels(key_of[10], (REQUEST_TOTAL, TOPK), ((0, 16),), -0.2, 0.2)), 0.05, 0.5)
    w_gate = scatter_about(key_of[11], (EXPERTS, D, HID), D ** -0.5, 0.125, ((0, 16), (2, 2)))
    w_up = scatter_about(key_of[12], (EXPERTS, D, HID), D ** -0.5, 0.125, ((0, 16), (2, 2)))
    w_down = scatter_about(key_of[13], (EXPERTS, D, HID), HID ** -0.5, 0.1875, ((0, 16), (2, 2)))
    return {"q_latent": q_latent, "latent_cache": latent_cache, "lengths": lengths, "residual": residual, "adapter_ids": adapter_ids, "value_out": value_out, "adapter_down": adapter_down, "adapter_up_factors": adapter_up_factors, "norm_gain": norm_gain, "expert_ids": expert_ids, "gate_weights": gate_weights, "w_gate": w_gate, "w_up": w_up, "w_down": w_down}


SOFTMAX_SCALE = 192.0 ** (-0.5)
ADAPTER_SCALE = 2.0
EPSILON = 1e-06

def attend_one(query, latent_rows, length):
    scores = jnp.dot(query, latent_rows.T, preferred_element_type=jnp.float32) * SOFTMAX_SCALE
    valid_mask = jnp.arange(latent_rows.shape[0], dtype=jnp.int32) < length
    scores = jnp.where(valid_mask[None, :], scores, -1e+30)
    row_max = lax.optimization_barrier(jnp.max(scores, axis=1, keepdims=True))
    raised = jnp.exp(scores - row_max)
    weights_bf = (raised / lax.optimization_barrier(jnp.sum(raised, axis=1, keepdims=True))).astype(jnp.bfloat16)
    return jnp.dot(weights_bf, latent_rows[:, :LAT], preferred_element_type=jnp.float32).astype(jnp.bfloat16)

def reference(q_latent, latent_cache, lengths, residual, adapter_ids, value_out, adapter_down, adapter_up_factors, norm_gain, expert_ids, gate_weights, w_gate, w_up, w_down):
    latent_out = lax.map(lambda packed: attend_one(packed[0], packed[1], packed[2]), (q_latent, latent_cache, lengths))
    latent_out = latent_out.reshape(REQUEST_TOTAL, HEADS * LAT)
    base_output = jnp.dot(latent_out, value_out, preferred_element_type=jnp.float32)
    down_projected_rows = jnp.dot(latent_out, adapter_down, preferred_element_type=jnp.float32).reshape(REQUEST_TOTAL, ADAPTER_TOTAL, ADAPTER_RANK)
    chosen_adapters = adapter_ids[:, None] == jnp.arange(ADAPTER_TOTAL, dtype=jnp.int32)[None, :]
    adapter_down_rows = lax.optimization_barrier(jnp.sum(jnp.where(chosen_adapters[:, :, None], down_projected_rows, 0.0), axis=1))
    adapter_scaled_output = (ADAPTER_SCALE * adapter_down_rows).astype(jnp.bfloat16)
    spread_rows = jnp.where(chosen_adapters[:, :, None], adapter_scaled_output[:, None, :], jnp.zeros((), jnp.bfloat16)).reshape(REQUEST_TOTAL, ADAPTER_TOTAL * ADAPTER_RANK)
    adapter_up_rows = jnp.dot(spread_rows, adapter_up_factors, preferred_element_type=jnp.float32)
    residual_flow = residual.astype(jnp.float32) + base_output + adapter_up_rows
    inverse_rms = lax.rsqrt(lax.optimization_barrier(jnp.mean(residual_flow * residual_flow, axis=1, keepdims=True)) + EPSILON)
    normed = (residual_flow * inverse_rms * norm_gain.astype(jnp.float32)).astype(jnp.bfloat16)
    load_bound = N_EXPERT * MOST
    padded = jnp.concatenate([normed, jnp.zeros((1, D), jnp.bfloat16)], axis=0)

    def one_expert(running, expert_index):
        hit_mask = expert_ids == expert_index
        member = jnp.any(hit_mask, axis=1)
        gate_sum = lax.optimization_barrier(jnp.sum(jnp.where(hit_mask, gate_weights, 0.0), axis=1))
        row_index = jnp.nonzero(member, size=load_bound, fill_value=REQUEST_TOTAL)[0].astype(jnp.int32)
        tokens = padded[row_index]
        gate_act = jnp.dot(tokens, w_gate[expert_index], preferred_element_type=jnp.float32)
        up_act = jnp.dot(tokens, w_up[expert_index], preferred_element_type=jnp.float32)
        hidden_bf = (jax.nn.silu(gate_act) * up_act).astype(jnp.bfloat16)
        produced = lax.dot_general(hidden_bf, w_down[expert_index], (((1,), (1,)), ((), ())), preferred_element_type=jnp.float32)
        gate_rows = jnp.concatenate([gate_sum, jnp.zeros((1,), gate_sum.dtype)])[row_index]
        running = running.at[row_index].add(gate_rows[:, None] * produced, mode='drop')
        return (running, None)
    routed, unused = lax.scan(one_expert, jnp.zeros((REQUEST_TOTAL, D), jnp.float32), jnp.arange(EXPERTS, dtype=jnp.int32))
    return (residual_flow + routed).astype(jnp.bfloat16)
```

```python
import functools

import jax
import jax.numpy as jnp
from jax import lax
from jax.experimental import pallas as pl
from jax.experimental.pallas import tpu as pltpu
from jax.sharding import PartitionSpec as P

LAT = 512
ADAPTER_RANK = 16
SOFTMAX_SCALE = 192.0 ** (-0.5)
ADAPTER_SCALE = 2.0
EPSILON = 1e-06
LANES = 128
MESH = pl.DeviceIdType.MESH
F32 = jnp.float32
BF16 = jnp.bfloat16
NT = (((1,), (1,)), ((), ()))
TN = (((0,), (0,)), ((), ()))


def layer_kernel(
    dims,
    lengths,
    adapter_ids,
    q_hbm,
    cache_hbm,
    residual_hbm,
    value_hbm,
    down_hbm,
    upf_hbm,
    gain_hbm,
    ids_hbm,
    gates_hbm,
    wg_hbm,
    wu_hbm,
    wd_hbm,
    out_ref,
    q,
    cache,
    residual,
    value_out,
    adapter_down,
    up_factors,
    gain,
    ids,
    gates,
    w_gate,
    w_up,
    w_down,
    meta,
    att,
    pieces,
    lora,
    rs1_out,
    rs1_in,
    tok,
    r1_out,
    r1_in,
    r2_out,
    r2_in,
    r3_out,
    r3_in,
    cache_sem,
    load_sem,
    send_sem,
    recv_sem,
    tok_sem,
):
    n_expert, n_dp, top = dims
    n_group = n_expert // 2
    me = lax.axis_index("expert")
    my_dp = lax.axis_index("dp")
    my_group = me // 2
    my_core = lax.rem(me, 2)
    other_core = 1 - my_core
    partner = my_group * 2 + other_core
    rows, model_width = residual.shape
    column = ids.shape[0]
    heads = q.shape[1]
    width = att.shape[2]
    group_rows = n_expert * rows
    lane_rows = lora.shape[2]

    cache_loads = []
    for r in range(rows):
        cache_loads.append(pltpu.make_async_copy(cache_hbm.at[r], cache.at[r], cache_sem.at[r]))
    small = []
    for k, (src, dst) in enumerate(
        (
            (q_hbm, q),
            (ids_hbm, ids),
            (gates_hbm, gates),
            (residual_hbm, residual),
            (gain_hbm, gain),
            (down_hbm, adapter_down),
            (value_hbm, value_out),
            (upf_hbm, up_factors),
            (wg_hbm, w_gate),
            (wu_hbm, w_up),
            (wd_hbm, w_down),
        )
    ):
        small.append(pltpu.make_async_copy(src, dst, load_sem.at[k]))
    small[0].start()
    for load in cache_loads:
        load.start()
    for load in small[1:]:
        load.start()

    barrier = pltpu.get_barrier_semaphore()
    for i in range(1, n_expert):
        pl.semaphore_signal(
            barrier, inc=1, device_id={"expert": lax.rem(me + i, n_expert)}, device_id_type=MESH
        )
    for i in range(1, n_dp):
        pl.semaphore_signal(
            barrier, inc=1, device_id={"dp": lax.rem(my_dp + i, n_dp)}, device_id_type=MESH
        )

    def send(src, dst, sends, recvs, where):
        pltpu.make_async_remote_copy(
            src_ref=src, dst_ref=dst, send_sem=sends, recv_sem=recvs, device_id=where,
            device_id_type=MESH,
        ).start()

    def wait_bytes(ref, sem):
        pltpu.make_async_copy(ref, ref, sem).wait()

    small[0].wait()
    outs = []
    for r in range(rows):
        cache_loads[r].wait()
        keys = cache[r]
        scores = lax.dot_general(q[r], keys, NT, preferred_element_type=F32) * SOFTMAX_SCALE
        position = lax.broadcasted_iota(jnp.int32, scores.shape, 1)
        scores = jnp.where(position < lengths[r], scores, -1e30)
        raised = jnp.exp(scores - jnp.max(scores, axis=1, keepdims=True))
        weights = (raised / jnp.sum(raised, axis=1, keepdims=True)).astype(BF16)
        outs.append(jnp.dot(weights, keys[:, :LAT], preferred_element_type=F32))
    by_head = jnp.stack(outs, axis=1).astype(BF16)
    parts = LAT // width
    if parts == 1:
        att[...] = by_head
    else:
        for h in range(heads):
            for part in range(parts):
                att[h * parts + part] = by_head[h, :, part * width : (part + 1) * width]

    small[1].wait()
    small[2].wait()
    lane = lax.broadcasted_iota(jnp.int32, (column, LANES), 1)
    dense = jnp.zeros((column, LANES), F32)
    for k in range(top):
        dense += jnp.where(lane == ids[:, k : k + 1], gates[:, k : k + 1], 0.0)
    meta[me, 0:column, :] = dense
    row_of = lax.broadcasted_iota(jnp.int32, (8, LANES), 0)
    named = jnp.zeros((8, LANES), jnp.int32)
    for r in range(rows):
        named = jnp.where(row_of == r, adapter_ids[r], named)
    meta[me, column : column + 8, :] = named.astype(F32)

    pl.semaphore_wait(barrier, n_expert - 1 + n_dp - 1)
    for i in range(1, n_expert):
        to = lax.rem(me + i, n_expert)
        send(att.at[to], pieces.at[me], send_sem.at[0], recv_sem.at[0], {"expert": to})
        mine = meta.at[me]
        send(mine, mine, send_sem.at[1], recv_sem.at[1], {"expert": to})
    pieces[me] = att[me]

    small[5].wait()
    wait_bytes(pieces.at[0 : n_expert - 1], recv_sem.at[0])
    latent = pieces[...].reshape(group_rows, width)
    wait_bytes(meta.at[0 : n_expert - 1], recv_sem.at[1])
    adapter_of = (
        meta[:, column : column + rows, :].reshape(group_rows, LANES)
    )
    full = jnp.dot(latent, adapter_down[...], preferred_element_type=F32)
    of_column = lax.broadcasted_iota(jnp.int32, full.shape, 1) // ADAPTER_RANK
    chosen = jnp.where(of_column.astype(F32) == adapter_of[:, 0:1], full, 0.0)
    high = chosen.astype(BF16)
    low = (chosen - high.astype(F32)).astype(BF16)
    fold_shape = (ADAPTER_RANK, full.shape[1])
    fold = (
        lax.rem(lax.broadcasted_iota(jnp.int32, fold_shape, 1), ADAPTER_RANK)
        == lax.broadcasted_iota(jnp.int32, fold_shape, 0)
    ).astype(F32).astype(BF16)
    down_part = lax.dot_general(fold, high, NT, preferred_element_type=F32) + lax.dot_general(
        fold, low, NT, preferred_element_type=F32
    )
    if lane_rows > group_rows:
        down_part = jnp.concatenate(
            [down_part, jnp.zeros((ADAPTER_RANK, lane_rows - group_rows), F32)], axis=1
        )
    lora[me] = down_part
    for i in range(1, n_expert):
        to = lax.rem(me + i, n_expert)
        send(lora.at[me], lora.at[me], send_sem.at[2], recv_sem.at[2], {"expert": to})

    small[6].wait()
    base = jnp.dot(latent, value_out[...], preferred_element_type=F32)
    small[7].wait()
    if lane_rows > group_rows:
        adapter_of = jnp.concatenate(
            [adapter_of, jnp.zeros((lane_rows - group_rows, LANES), F32)], axis=0
        )
    adapter_lane = adapter_of.T[0:1, :]
    wait_bytes(lora.at[0 : n_expert - 1], recv_sem.at[2])
    scaled = (ADAPTER_SCALE * jnp.sum(lora[...], axis=0)).astype(BF16).astype(F32)
    owned = up_factors.shape[0] // ADAPTER_RANK
    spread = []
    for o in range(owned):
        holds = adapter_lane == (me * owned + o).astype(F32)
        spread.append(jnp.where(holds, scaled, 0.0))
    spread = jnp.concatenate(spread, axis=0).astype(BF16)[:, :group_rows]
    base += lax.dot_general(spread, up_factors[...], TN, preferred_element_type=F32)
    rs1_out[...] = base.reshape(n_expert, rows, model_width).astype(BF16)
    for i in range(1, n_expert):
        to = lax.rem(me + i, n_expert)
        send(rs1_out.at[to], rs1_in.at[me], send_sem.at[3], recv_sem.at[3], {"expert": to})
    rs1_in[me] = rs1_out[me]
    small[3].wait()
    small[4].wait()
    wait_bytes(rs1_in.at[0 : n_expert - 1], recv_sem.at[3])
    attention = jnp.sum(rs1_in[...].astype(F32), axis=0)
    stream = residual[...].astype(F32) + attention
    inverse_rms = lax.rsqrt(jnp.mean(stream * stream, axis=1, keepdims=True) + EPSILON)
    normed = stream * inverse_rms * gain[...].astype(F32)
    tok[my_core, my_dp, my_group] = normed.astype(BF16)

    def block(core, dp, group):
        return tok.at[core, dp, group], tok_sem.at[dp * n_group + group]

    own, own_sem = block(my_core, my_dp, my_group)
    for i in range(1, n_group):
        to = lax.rem(my_group + i, n_group) * 2 + my_core
        send(own, own, send_sem.at[4], own_sem, {"expert": to})
    for i in range(n_group):
        group = lax.rem(my_group + n_group - i, n_group)
        here, here_sem = block(my_core, my_dp, group)
        if i > 0:
            wait_bytes(here, here_sem)
        for j in range(1, n_dp):
            send(here, here, send_sem.at[5], here_sem, {"dp": lax.rem(my_dp + j, n_dp)})
        send(here, here, send_sem.at[6], recv_sem.at[4], {"expert": partner})
    for j in range(1, n_dp):
        from_dp = lax.rem(my_dp + n_dp - j, n_dp)
        for i in range(n_group):
            group = lax.rem(my_group + n_group - i, n_group)
            here, here_sem = block(my_core, from_dp, group)
            wait_bytes(here, here_sem)
            send(here, here, send_sem.at[6], recv_sem.at[4], {"expert": partner})

    def produce(core):
        tokens = tok[core].reshape(n_dp * n_group * rows, model_width)
        weight = []
        for dp in range(n_dp):
            of_rows = meta[pl.ds(core, n_group, stride=2), dp * rows : (dp + 1) * rows, :]
            of_rows = of_rows.reshape(n_group * rows, LANES)
            lanes = lax.broadcasted_iota(jnp.int32, of_rows.shape, 1)
            weight.append(jnp.sum(jnp.where(lanes == me, of_rows, 0.0), axis=1, keepdims=True))
        weight = jnp.concatenate(weight, axis=0)
        gate_act = jnp.dot(tokens, w_gate[0], preferred_element_type=F32)
        up_act = jnp.dot(tokens, w_up[0], preferred_element_type=F32)
        hidden = (gate_act / (1.0 + jnp.exp(-gate_act)) * up_act).astype(BF16)
        made = lax.dot_general(hidden, w_down[0], NT, preferred_element_type=F32)
        return (made * weight).reshape(n_dp, n_group, rows, model_width)

    for k in (8, 9, 10):
        small[k].wait()
    wait_bytes(tok.at[0], recv_sem.at[4])
    r1_out[...] = produce(other_core).astype(BF16)
    send(r1_out, r1_in, send_sem.at[7], recv_sem.at[5], {"expert": partner})
    kept = produce(my_core)
    r2_out[...] = kept.astype(BF16)
    wait_bytes(r1_in, recv_sem.at[5])
    r2_out[...] = (r2_out[...].astype(F32) + r1_in[...].astype(F32)).astype(BF16)
    for j in range(1, n_dp):
        to = lax.rem(my_dp + j, n_dp)
        send(r2_out.at[to], r2_in.at[my_dp], send_sem.at[8], recv_sem.at[6], {"dp": to})
    r2_in[my_dp] = r2_out[my_dp]
    if n_dp > 1:
        wait_bytes(r2_in.at[0 : n_dp - 1], recv_sem.at[6])
    r3_out[...] = jnp.sum(r2_in[...].astype(F32), axis=0).astype(BF16)
    for i in range(1, n_group):
        to = lax.rem(my_group + i, n_group)
        send(
            r3_out.at[to], r3_in.at[my_group], send_sem.at[9], recv_sem.at[7],
            {"expert": to * 2 + my_core},
        )
    r3_in[my_group] = r3_out[my_group]
    wait_bytes(r3_in.at[0 : n_group - 1], recv_sem.at[7])
    routed = jnp.sum(r3_in[...].astype(F32), axis=0)
    out_ref[...] = (stream + routed).astype(BF16)

    wait_bytes(att.at[0 : n_expert - 1], send_sem.at[0])
    wait_bytes(meta.at[0 : n_expert - 1], send_sem.at[1])
    wait_bytes(lora.at[0 : n_expert - 1], send_sem.at[2])
    wait_bytes(rs1_out.at[0 : n_expert - 1], send_sem.at[3])
    wait_bytes(tok.at[0, 0, 0 : n_group - 1], send_sem.at[4])
    if n_dp > 1:
        wait_bytes(tok.at[0, 0 : n_dp - 1], send_sem.at[5])
        wait_bytes(r2_out.at[0 : n_dp - 1], send_sem.at[8])
    wait_bytes(tok.at[0], send_sem.at[6])
    wait_bytes(r1_out, send_sem.at[7])
    wait_bytes(r3_out.at[0 : n_group - 1], send_sem.at[9])


def local(
    n_expert,
    n_dp,
    q_latent,
    latent_cache,
    lengths,
    residual,
    adapter_ids,
    value_out,
    adapter_down,
    adapter_up_factors,
    norm_gain,
    expert_ids,
    gate_weights,
    w_gate,
    w_up,
    w_down,
):
    rows, model_width = residual.shape
    column, top = expert_ids.shape
    heads = q_latent.shape[1]
    width = heads * LAT // n_expert
    n_group = n_expert // 2
    lane_rows = -(-n_expert * rows // LANES) * LANES
    gain = norm_gain.reshape(1, model_width)
    big = (
        q_latent,
        latent_cache,
        residual,
        value_out,
        adapter_down,
        adapter_up_factors,
        gain,
        expert_ids,
        gate_weights,
        w_gate,
        w_up,
        w_down,
    )
    any_spec = pl.BlockSpec(memory_space=pl.ANY)
    smem_spec = pl.BlockSpec(memory_space=pltpu.SMEM)
    dma = pltpu.SemaphoreType.DMA
    all_rows = (n_dp, n_group, rows, model_width)
    return pl.pallas_call(
        functools.partial(layer_kernel, (n_expert, n_dp, top)),
        out_shape=jax.ShapeDtypeStruct((rows, model_width), BF16),
        in_specs=[smem_spec] * 2 + [any_spec] * len(big),
        out_specs=pl.BlockSpec(memory_space=pltpu.VMEM),
        scratch_shapes=[pltpu.VMEM(a.shape, a.dtype) for a in big]
        + [
            pltpu.VMEM((n_expert, column + 8, LANES), F32),
            pltpu.VMEM((n_expert, rows, width), BF16),
            pltpu.VMEM((n_expert, rows, width), BF16),
            pltpu.VMEM((n_expert, ADAPTER_RANK, lane_rows), F32),
            pltpu.VMEM((n_expert, rows, model_width), BF16),
            pltpu.VMEM((n_expert, rows, model_width), BF16),
            pltpu.VMEM((2,) + all_rows, BF16),
            pltpu.VMEM(all_rows, BF16),
            pltpu.VMEM(all_rows, BF16),
            pltpu.VMEM(all_rows, BF16),
            pltpu.VMEM(all_rows, BF16),
            pltpu.VMEM(all_rows[1:], BF16),
            pltpu.VMEM(all_rows[1:], BF16),
            dma((rows,)),
            dma((11,)),
            dma((10,)),
            dma((8,)),
            dma((n_dp * n_group,)),
        ],
        compiler_params=pltpu.CompilerParams(
            collective_id=0, has_side_effects=True, vmem_limit_bytes=64000000
        ),
        name="layer",
    )(lengths, adapter_ids, *big)


def solution(mesh):
    in_specs = (
        P(("expert", "dp"), None, None),
        P(("expert", "dp"), None, None),
        P(("expert", "dp")),
        P(("expert", "dp"), None),
        P(("expert", "dp")),
        P("expert", None),
        P("expert", None),
        P("expert", None),
        P(),
        P("expert", None),
        P("expert", None),
        P("expert", None, "dp"),
        P("expert", None, "dp"),
        P("expert", None, "dp"),
    )
    return jax.shard_map(
        functools.partial(local, mesh.shape["expert"], mesh.shape["dp"]),
        mesh=mesh,
        in_specs=in_specs,
        out_specs=P(("expert", "dp"), None),
        check_vma=False,
    )
```

```python
import functools

import jax
import jax.numpy as jnp
from jax import lax
from jax.experimental import pallas as pl
from jax.experimental.pallas import tpu as pltpu
from jax.sharding import PartitionSpec as P

LAT = 512
ADAPTER_RANK = 16
SOFTMAX_SCALE = 192.0 ** (-0.5)
ADAPTER_SCALE = 2.0
EPSILON = 1e-06
LANES = 128
CHUNKS = 4
MESH = pl.DeviceIdType.MESH
F32 = jnp.float32
BF16 = jnp.bfloat16
NT = (((1,), (1,)), ((), ()))
TN = (((0,), (0,)), ((), ()))


def layer_kernel(
    dims,
    lengths,
    adapter_ids,
    q_hbm,
    cache_hbm,
    residual_hbm,
    value_hbm,
    down_hbm,
    upf_hbm,
    gain_hbm,
    ids_hbm,
    gates_hbm,
    wg_hbm,
    wu_hbm,
    wd_hbm,
    out_ref,
    q,
    cache,
    residual,
    value_out,
    adapter_down,
    up_factors,
    gain,
    ids,
    gates,
    w_gate,
    w_up,
    w_down,
    names,
    dense_gates,
    att,
    pieces,
    lora,
    a1_out,
    a1_in,
    a2_out,
    a2_in,
    tok,
    r1_out,
    r1_in,
    r2_out,
    r2_in,
    r3_out,
    r3_in,
    cache_sem,
    load_sem,
    send_sem,
    recv_sem,
    tok_sem,
    chunk_send,
    chunk_recv,
):
    n_expert, n_dp, top = dims
    n_group = n_expert // 2
    me = lax.axis_index("expert")
    my_dp = lax.axis_index("dp")
    my_group = me // 2
    my_core = lax.rem(me, 2)
    other_core = 1 - my_core
    partner = my_group * 2 + other_core
    rows, model_width = residual.shape
    column = ids.shape[0]
    heads = q.shape[1]
    width = att.shape[2]
    group_rows = n_expert * rows
    chunks = a1_out.shape[0]
    chunk = model_width // chunks
    packed = ADAPTER_RANK // lora.shape[1]

    cache_loads = []
    for r in range(rows):
        cache_loads.append(pltpu.make_async_copy(cache_hbm.at[r], cache.at[r], cache_sem.at[r]))
    small = []
    for k, (src, dst) in enumerate(
        (
            (q_hbm, q),
            (ids_hbm, ids),
            (gates_hbm, gates),
            (residual_hbm, residual),
            (gain_hbm, gain),
            (down_hbm, adapter_down),
            (value_hbm, value_out),
            (upf_hbm, up_factors),
            (wg_hbm, w_gate),
            (wu_hbm, w_up),
            (wd_hbm, w_down),
        )
    ):
        small.append(pltpu.make_async_copy(src, dst, load_sem.at[k]))
    small[0].start()
    for load in cache_loads:
        load.start()
    for load in small[1:]:
        load.start()

    barrier = pltpu.get_barrier_semaphore()
    for i in range(1, n_expert):
        pl.semaphore_signal(
            barrier, inc=1, device_id={"expert": lax.rem(me + i, n_expert)}, device_id_type=MESH
        )
    for i in range(1, n_dp):
        pl.semaphore_signal(
            barrier, inc=1, device_id={"dp": lax.rem(my_dp + i, n_dp)}, device_id_type=MESH
        )

    def send(src, dst, sends, recvs, where):
        pltpu.make_async_remote_copy(
            src_ref=src, dst_ref=dst, send_sem=sends, recv_sem=recvs, device_id=where,
            device_id_type=MESH,
        ).start()

    def wait_bytes(ref, sem):
        pltpu.make_async_copy(ref, ref, sem).wait()

    small[0].wait()
    outs = []
    for r in range(rows):
        cache_loads[r].wait()
        keys = cache[r]
        scores = jnp.dot(q[r], keys, preferred_element_type=F32) * SOFTMAX_SCALE
        position = lax.broadcasted_iota(jnp.int32, scores.shape, 1)
        scores = jnp.where(position < lengths[r], scores, -1e30)
        raised = jnp.exp(scores - jnp.max(scores, axis=1, keepdims=True))
        weights = (raised / jnp.sum(raised, axis=1, keepdims=True)).astype(BF16)
        outs.append(lax.dot_general(weights, keys[:LAT], NT, preferred_element_type=F32))
    by_head = jnp.stack(outs, axis=1).astype(BF16)
    parts = LAT // width
    if parts == 1:
        att[...] = by_head
    else:
        for h in range(heads):
            for part in range(parts):
                att[h * parts + part] = by_head[h, :, part * width : (part + 1) * width]

    pl.semaphore_wait(barrier, n_expert - 1 + n_dp - 1)
    peers = [lax.rem(me + i, n_expert) for i in range(1, n_expert)]
    for to in peers:
        send(att.at[to], pieces.at[me], send_sem.at[0], recv_sem.at[0], {"expert": to})
    row_of = lax.broadcasted_iota(jnp.int32, (rows, LANES), 0)
    named = jnp.zeros((rows, LANES), jnp.int32)
    for r in range(rows):
        named = jnp.where(row_of == r, adapter_ids[r], named)
    names[me] = named.astype(F32)
    for to in peers:
        send(names.at[me], names.at[me], send_sem.at[1], recv_sem.at[1], {"expert": to})
    pieces[me] = att[me]

    small[5].wait()
    fold_shape = (ADAPTER_RANK, adapter_down.shape[1])
    fold = (
        lax.rem(lax.broadcasted_iota(jnp.int32, fold_shape, 1), ADAPTER_RANK)
        == lax.broadcasted_iota(jnp.int32, fold_shape, 0)
    ).astype(F32).astype(BF16)
    wait_bytes(pieces.at[0 : n_expert - 1], recv_sem.at[0])
    latent = pieces[...].reshape(group_rows, width)
    full = jnp.dot(latent, adapter_down[...], preferred_element_type=F32)
    of_column = lax.broadcasted_iota(jnp.int32, full.shape, 1) // ADAPTER_RANK
    wait_bytes(names.at[0 : n_expert - 1], recv_sem.at[1])
    adapter_of = names[...].reshape(group_rows, LANES)
    chosen = jnp.where(of_column.astype(F32) == adapter_of[:, 0:1], full, 0.0)
    high = chosen.astype(BF16)
    low = (chosen - high.astype(F32)).astype(BF16)
    down_part = lax.dot_general(fold, high, NT, preferred_element_type=F32) + lax.dot_general(
        fold, low, NT, preferred_element_type=F32
    )
    if packed == 2:
        half = ADAPTER_RANK // 2
        down_part = jnp.concatenate([down_part[:half], down_part[half:]], axis=1)
    lora[me] = down_part
    for to in peers:
        send(lora.at[me], lora.at[me], send_sem.at[2], recv_sem.at[2], {"expert": to})

    small[1].wait()
    small[2].wait()
    lane = lax.broadcasted_iota(jnp.int32, (column, LANES), 1)
    dense = jnp.zeros((column, LANES), F32)
    for k in range(top):
        dense += jnp.where(lane == ids[:, k : k + 1], gates[:, k : k + 1], 0.0)
    dense_gates[me] = dense
    for to in peers:
        mine = dense_gates.at[me]
        send(mine, mine, send_sem.at[3], recv_sem.at[3], {"expert": to})

    small[6].wait()
    base = jnp.dot(latent, value_out[...], preferred_element_type=F32)
    small[7].wait()
    small[3].wait()
    small[4].wait()
    pad_rows = -group_rows % LANES
    if pad_rows:
        adapter_of = jnp.concatenate([adapter_of, jnp.zeros((pad_rows, LANES), F32)], axis=0)
    adapter_lane = adapter_of.T[0:1, :group_rows]
    wait_bytes(lora.at[0 : n_expert - 1], recv_sem.at[2])
    scaled = (ADAPTER_SCALE * jnp.sum(lora[...], axis=0)).astype(BF16).astype(F32)
    if packed == 2:
        scaled = jnp.concatenate([scaled[:, :group_rows], scaled[:, group_rows:]], axis=0)
    owned = up_factors.shape[0] // ADAPTER_RANK
    spread = []
    for o in range(owned):
        holds = adapter_lane == (me * owned + o).astype(F32)
        spread.append(jnp.where(holds, scaled, 0.0))
    spread = jnp.concatenate(spread, axis=0).astype(BF16)

    groups = [lax.rem(my_group + i, n_group) for i in range(1, n_group)]
    for k in range(chunks):
        columns = slice(k * chunk, (k + 1) * chunk)
        projected = base[:, columns] + lax.dot_general(
            spread, up_factors[:, columns], TN, preferred_element_type=F32
        )
        projected = projected.reshape(n_group, 2, rows, chunk).astype(BF16)
        for core in range(2):
            a1_out[k, core] = projected[:, core]
        send(
            a1_out.at[k, other_core], a1_in.at[k], chunk_send.at[0, k], chunk_recv.at[0, k],
            {"expert": partner},
        )
    for k in range(chunks):
        wait_bytes(a1_in.at[k], chunk_recv.at[0, k])
        a2_out[k] = (a1_out[k, my_core].astype(F32) + a1_in[k].astype(F32)).astype(BF16)
        for to in groups:
            send(
                a2_out.at[k, to], a2_in.at[k, my_group], chunk_send.at[1, k], chunk_recv.at[1, k],
                {"expert": to * 2 + my_core},
            )
        a2_in[k, my_group] = a2_out[k, my_group]
    attention = []
    for k in range(chunks):
        wait_bytes(a2_in.at[k, 0 : n_group - 1], chunk_recv.at[1, k])
        attention.append(jnp.sum(a2_in[k].astype(F32), axis=0))
    stream = residual[...].astype(F32) + jnp.concatenate(attention, axis=1)
    inverse_rms = lax.rsqrt(jnp.mean(stream * stream, axis=1, keepdims=True) + EPSILON)
    normed = stream * inverse_rms * gain[...].reshape(1, model_width).astype(F32)
    tok[my_core, my_dp, my_group] = normed.astype(BF16)

    def block(core, dp, group):
        return tok.at[core, dp, group], tok_sem.at[dp * n_group + group]

    own, own_sem = block(my_core, my_dp, my_group)
    for i in range(1, n_group):
        to = lax.rem(my_group + i, n_group) * 2 + my_core
        send(own, own, send_sem.at[4], own_sem, {"expert": to})
    for i in range(n_group):
        group = lax.rem(my_group + n_group - i, n_group)
        here, here_sem = block(my_core, my_dp, group)
        if i > 0:
            wait_bytes(here, here_sem)
        for j in range(1, n_dp):
            send(here, here, send_sem.at[5], here_sem, {"dp": lax.rem(my_dp + j, n_dp)})
        send(here, here, send_sem.at[6], recv_sem.at[4], {"expert": partner})
    for j in range(1, n_dp):
        from_dp = lax.rem(my_dp + n_dp - j, n_dp)
        for i in range(n_group):
            group = lax.rem(my_group + n_group - i, n_group)
            here, here_sem = block(my_core, from_dp, group)
            wait_bytes(here, here_sem)
            send(here, here, send_sem.at[6], recv_sem.at[4], {"expert": partner})

    all_rows = 2 * n_dp * n_group * rows
    wait_bytes(dense_gates.at[0 : n_expert - 1], recv_sem.at[3])
    weight = []
    for core in range(2):
        for dp in range(n_dp):
            of_rows = dense_gates[
                pl.ds(core, n_group, stride=2), dp * rows : (dp + 1) * rows, :
            ].reshape(n_group * rows, LANES)
            lanes = lax.broadcasted_iota(jnp.int32, of_rows.shape, 1)
            weight.append(jnp.sum(jnp.where(lanes == me, of_rows, 0.0), axis=1, keepdims=True))
    weight = jnp.concatenate(weight, axis=0)
    for k in (8, 9, 10):
        small[k].wait()
    wait_bytes(tok.at[0], recv_sem.at[4])
    tokens = tok[...].reshape(all_rows, model_width)
    gate_act = jnp.dot(tokens, w_gate[0], preferred_element_type=F32)
    up_act = jnp.dot(tokens, w_up[0], preferred_element_type=F32)
    hidden = (gate_act / (1.0 + jnp.exp(-gate_act)) * up_act).astype(BF16)

    for k in range(chunks):
        made = lax.dot_general(
            hidden, w_down[0, k * chunk : (k + 1) * chunk, :], NT, preferred_element_type=F32
        )
        r1_out[k] = (made * weight).reshape(2, n_dp, n_group, rows, chunk).astype(BF16)
        send(
            r1_out.at[k, other_core], r1_in.at[k], chunk_send.at[2, k], chunk_recv.at[2, k],
            {"expert": partner},
        )
    for k in range(chunks):
        wait_bytes(r1_in.at[k], chunk_recv.at[2, k])
        r2_out[k] = (r1_out[k, my_core].astype(F32) + r1_in[k].astype(F32)).astype(BF16)
        for j in range(1, n_dp):
            to = lax.rem(my_dp + j, n_dp)
            send(
                r2_out.at[k, to], r2_in.at[k, my_dp], chunk_send.at[3, k], chunk_recv.at[3, k],
                {"dp": to},
            )
        r2_in[k, my_dp] = r2_out[k, my_dp]
    for k in range(chunks):
        if n_dp > 1:
            wait_bytes(r2_in.at[k, 0 : n_dp - 1], chunk_recv.at[3, k])
        r3_out[k] = jnp.sum(r2_in[k].astype(F32), axis=0).astype(BF16)
        for to in groups:
            send(
                r3_out.at[k, to], r3_in.at[k, my_group], chunk_send.at[4, k], chunk_recv.at[4, k],
                {"expert": to * 2 + my_core},
            )
        r3_in[k, my_group] = r3_out[k, my_group]
    for k in range(chunks):
        wait_bytes(r3_in.at[k, 0 : n_group - 1], chunk_recv.at[4, k])
        routed = jnp.sum(r3_in[k].astype(F32), axis=0)
        columns = slice(k * chunk, (k + 1) * chunk)
        out_ref[:, columns] = (stream[:, columns] + routed).astype(BF16)

    for k, ref in enumerate((att, names, lora, dense_gates)):
        wait_bytes(ref.at[0 : n_expert - 1], send_sem.at[k])
    wait_bytes(tok.at[0, 0, 0 : n_group - 1], send_sem.at[4])
    if n_dp > 1:
        wait_bytes(tok.at[0, 0 : n_dp - 1], send_sem.at[5])
    wait_bytes(tok.at[0], send_sem.at[6])
    for k in range(chunks):
        wait_bytes(a1_in.at[k], chunk_send.at[0, k])
        wait_bytes(a2_out.at[k, 0 : n_group - 1], chunk_send.at[1, k])
        wait_bytes(r1_in.at[k], chunk_send.at[2, k])
        if n_dp > 1:
            wait_bytes(r2_out.at[k, 0 : n_dp - 1], chunk_send.at[3, k])
        wait_bytes(r3_out.at[k, 0 : n_group - 1], chunk_send.at[4, k])


def local(
    n_expert,
    n_dp,
    q_latent,
    latent_cache,
    lengths,
    residual,
    adapter_ids,
    value_out,
    adapter_down,
    adapter_up_factors,
    norm_gain,
    expert_ids,
    gate_weights,
    w_gate,
    w_up,
    w_down,
):
    rows, model_width = residual.shape
    column, top = expert_ids.shape
    heads = q_latent.shape[1]
    width = heads * LAT // n_expert
    n_group = n_expert // 2
    packed = 2 if n_expert * rows * 2 == LANES else 1
    lane_rows = packed * n_expert * rows
    chunks = CHUNKS
    chunk = model_width // chunks
    big = (
        q_latent,
        latent_cache.swapaxes(1, 2),
        residual,
        value_out,
        adapter_down,
        adapter_up_factors,
        norm_gain,
        expert_ids,
        gate_weights,
        w_gate,
        w_up,
        w_down,
    )
    any_spec = pl.BlockSpec(memory_space=pl.ANY)
    smem_spec = pl.BlockSpec(memory_space=pltpu.SMEM)
    dma = pltpu.SemaphoreType.DMA
    to_groups = (n_group, rows, chunk)
    to_all = (n_dp,) + to_groups
    return pl.pallas_call(
        functools.partial(layer_kernel, (n_expert, n_dp, top)),
        out_shape=jax.ShapeDtypeStruct((rows, model_width), BF16),
        in_specs=[smem_spec] * 2 + [any_spec] * len(big),
        out_specs=pl.BlockSpec(memory_space=pltpu.VMEM),
        scratch_shapes=[pltpu.VMEM(a.shape, a.dtype) for a in big]
        + [
            pltpu.VMEM((n_expert, rows, LANES), F32),
            pltpu.VMEM((n_expert, column, LANES), F32),
            pltpu.VMEM((n_expert, rows, width), BF16),
            pltpu.VMEM((n_expert, rows, width), BF16),
            pltpu.VMEM((n_expert, ADAPTER_RANK // packed, lane_rows), F32),
            pltpu.VMEM((chunks, 2) + to_groups, BF16),
            pltpu.VMEM((chunks,) + to_groups, BF16),
            pltpu.VMEM((chunks,) + to_groups, BF16),
            pltpu.VMEM((chunks,) + to_groups, BF16),
            pltpu.VMEM((2, n_dp, n_group, rows, model_width), BF16),
            pltpu.VMEM((chunks, 2) + to_all, BF16),
            pltpu.VMEM((chunks,) + to_all, BF16),
            pltpu.VMEM((chunks,) + to_all, BF16),
            pltpu.VMEM((chunks,) + to_all, BF16),
            pltpu.VMEM((chunks,) + to_groups, BF16),
            pltpu.VMEM((chunks,) + to_groups, BF16),
            dma((rows,)),
            dma((11,)),
            dma((10,)),
            dma((8,)),
            dma((n_dp * n_group,)),
            dma((5, chunks)),
            dma((5, chunks)),
        ],
        compiler_params=pltpu.CompilerParams(
            collective_id=0, has_side_effects=True, vmem_limit_bytes=64000000
        ),
        name="layer",
    )(lengths, adapter_ids, *big)


def solution(mesh):
    in_specs = (
        P(("expert", "dp"), None, None),
        P(("expert", "dp"), None, None),
        P(("expert", "dp")),
        P(("expert", "dp"), None),
        P(("expert", "dp")),
        P("expert", None),
        P("expert", None),
        P("expert", None),
        P(),
        P("expert", None),
        P("expert", None),
        P("expert", None, "dp"),
        P("expert", None, "dp"),
        P("expert", None, "dp"),
    )
    return jax.shard_map(
        functools.partial(local, mesh.shape["expert"], mesh.shape["dp"]),
        mesh=mesh,
        in_specs=in_specs,
        out_specs=P(("expert", "dp"), None),
        check_vma=False,
    )
```

```python
import functools

import jax
import jax.numpy as jnp
from jax import lax
from jax.experimental import pallas as pl
from jax.experimental.pallas import tpu as pltpu
from jax.sharding import PartitionSpec as P

LAT = 512
ADAPTER_RANK = 16
SOFTMAX_SCALE = 192.0 ** (-0.5)
ADAPTER_SCALE = 2.0
EPSILON = 1e-06
LANES = 128
CHUNKS = 4
MESH = pl.DeviceIdType.MESH
F32 = jnp.float32
BF16 = jnp.bfloat16
NT = (((1,), (1,)), ((), ()))
TN = (((0,), (0,)), ((), ()))


def layer_kernel(
    dims,
    lengths,
    adapter_ids,
    q_hbm,
    cache_hbm,
    residual_hbm,
    value_hbm,
    down_hbm,
    upf_hbm,
    gain_hbm,
    ids_hbm,
    gates_hbm,
    wg_hbm,
    wu_hbm,
    wd_hbm,
    out_ref,
    q,
    cache,
    residual,
    value_out,
    adapter_down,
    up_factors,
    gain,
    ids,
    gates,
    w_gate,
    w_up,
    w_down,
    names,
    dense_gates,
    att,
    pieces,
    lora,
    a1_out,
    a1_in,
    a2_out,
    a2_in,
    tok,
    r1_out,
    r1_in,
    r2_out,
    r2_in,
    r3_out,
    r3_in,
    cache_sem,
    load_sem,
    send_sem,
    recv_sem,
    tok_sem,
    chunk_send,
    chunk_recv,
):
    n_expert, n_dp, top = dims
    n_group = n_expert // 2
    me = lax.axis_index("expert")
    my_dp = lax.axis_index("dp")
    my_group = me // 2
    my_core = lax.rem(me, 2)
    other_core = 1 - my_core
    partner = my_group * 2 + other_core
    rows, model_width = residual.shape
    column = ids.shape[0]
    heads = q.shape[1]
    width = att.shape[2]
    group_rows = n_expert * rows
    chunks = a1_out.shape[0]
    chunk = model_width // chunks
    packed = ADAPTER_RANK // lora.shape[1]

    cache_loads = []
    for r in range(rows):
        cache_loads.append(pltpu.make_async_copy(cache_hbm.at[r], cache.at[r], cache_sem.at[r]))
    small = []
    for k, (src, dst) in enumerate(
        (
            (q_hbm, q),
            (ids_hbm, ids),
            (gates_hbm, gates),
            (residual_hbm, residual),
            (gain_hbm, gain),
            (down_hbm, adapter_down),
            (value_hbm, value_out),
            (upf_hbm, up_factors),
            (wg_hbm, w_gate),
            (wu_hbm, w_up),
            (wd_hbm, w_down),
        )
    ):
        small.append(pltpu.make_async_copy(src, dst, load_sem.at[k]))
    small[0].start()
    for load in cache_loads:
        load.start()

    barrier = pltpu.get_barrier_semaphore()
    for i in range(1, n_expert):
        pl.semaphore_signal(
            barrier, inc=1, device_id={"expert": lax.rem(me + i, n_expert)}, device_id_type=MESH
        )
    for i in range(1, n_dp):
        pl.semaphore_signal(
            barrier, inc=1, device_id={"dp": lax.rem(my_dp + i, n_dp)}, device_id_type=MESH
        )

    def send(src, dst, sends, recvs, where):
        pltpu.make_async_remote_copy(
            src_ref=src, dst_ref=dst, send_sem=sends, recv_sem=recvs, device_id=where,
            device_id_type=MESH,
        ).start()

    def wait_bytes(ref, sem):
        pltpu.make_async_copy(ref, ref, sem).wait()

    small[0].wait()
    for load in cache_loads:
        load.wait()
    for k in (5, 6, 7, 1, 2, 3, 4, 8, 9, 10):
        small[k].start()
    all_scores = []
    for r in range(rows):
        scores = jnp.dot(q[r], cache[r], preferred_element_type=F32) * SOFTMAX_SCALE
        position = lax.broadcasted_iota(jnp.int32, scores.shape, 1)
        all_scores.append(jnp.where(position < lengths[r], scores, -1e30))
    all_scores = jnp.concatenate(all_scores, axis=0)
    raised = jnp.exp(all_scores - jnp.max(all_scores, axis=1, keepdims=True))
    weights = (raised / jnp.sum(raised, axis=1, keepdims=True)).astype(BF16)

    row_of = lax.broadcasted_iota(jnp.int32, (rows, LANES), 0)
    named = jnp.zeros((rows, LANES), jnp.int32)
    for r in range(rows):
        named = jnp.where(row_of == r, adapter_ids[r], named)
    names[me] = named.astype(F32)
    peers = [lax.rem(me + i, n_expert) for i in range(1, n_expert)]
    pl.semaphore_wait(barrier, n_expert - 1 + n_dp - 1)
    for to in peers:
        send(names.at[me], names.at[me], send_sem.at[1], recv_sem.at[1], {"expert": to})
    outs = []
    for r in range(rows):
        of_request = weights[r * heads : (r + 1) * heads]
        outs.append(
            lax.dot_general(of_request, cache[r, :LAT], NT, preferred_element_type=F32)
        )
    by_head = jnp.stack(outs, axis=1).astype(BF16)
    parts = LAT // width
    if parts == 1:
        att[...] = by_head
    else:
        for h in range(heads):
            for part in range(parts):
                att[h * parts + part] = by_head[h, :, part * width : (part + 1) * width]

    for to in peers:
        send(att.at[to], pieces.at[me], send_sem.at[0], recv_sem.at[0], {"expert": to})
    pieces[me] = att[me]

    small[5].wait()
    fold_shape = (ADAPTER_RANK, adapter_down.shape[1])
    fold = (
        lax.rem(lax.broadcasted_iota(jnp.int32, fold_shape, 1), ADAPTER_RANK)
        == lax.broadcasted_iota(jnp.int32, fold_shape, 0)
    ).astype(F32).astype(BF16)
    wait_bytes(pieces.at[0 : n_expert - 1], recv_sem.at[0])
    latent = pieces[...].reshape(group_rows, width)
    full = jnp.dot(latent, adapter_down[...], preferred_element_type=F32)
    of_column = lax.broadcasted_iota(jnp.int32, full.shape, 1) // ADAPTER_RANK
    wait_bytes(names.at[0 : n_expert - 1], recv_sem.at[1])
    adapter_of = names[...].reshape(group_rows, LANES)
    chosen = jnp.where(of_column.astype(F32) == adapter_of[:, 0:1], full, 0.0)
    high = chosen.astype(BF16)
    low = (chosen - high.astype(F32)).astype(BF16)
    down_part = lax.dot_general(fold, high, NT, preferred_element_type=F32) + lax.dot_general(
        fold, low, NT, preferred_element_type=F32
    )
    if packed == 2:
        half = ADAPTER_RANK // 2
        down_part = jnp.concatenate([down_part[:half], down_part[half:]], axis=1)
    lora[me] = down_part
    for to in peers:
        send(lora.at[me], lora.at[me], send_sem.at[2], recv_sem.at[2], {"expert": to})

    small[1].wait()
    small[2].wait()
    lane = lax.broadcasted_iota(jnp.int32, (column, LANES), 1)
    dense = jnp.zeros((column, LANES), F32)
    for k in range(top):
        dense += jnp.where(lane == ids[:, k : k + 1], gates[:, k : k + 1], 0.0)
    dense_gates[me] = dense
    for to in peers:
        mine = dense_gates.at[me]
        send(mine, mine, send_sem.at[3], recv_sem.at[3], {"expert": to})

    small[6].wait()
    base = jnp.dot(latent, value_out[...], preferred_element_type=F32)
    small[7].wait()
    small[3].wait()
    small[4].wait()
    pad_rows = -group_rows % LANES
    if pad_rows:
        adapter_of = jnp.concatenate([adapter_of, jnp.zeros((pad_rows, LANES), F32)], axis=0)
    adapter_lane = adapter_of.T[0:1, :group_rows]
    wait_bytes(lora.at[0 : n_expert - 1], recv_sem.at[2])
    scaled = (ADAPTER_SCALE * jnp.sum(lora[...], axis=0)).astype(BF16).astype(F32)
    if packed == 2:
        scaled = jnp.concatenate([scaled[:, :group_rows], scaled[:, group_rows:]], axis=0)
    owned = up_factors.shape[0] // ADAPTER_RANK
    spread = []
    for o in range(owned):
        holds = adapter_lane == (me * owned + o).astype(F32)
        spread.append(jnp.where(holds, scaled, 0.0))
    spread = jnp.concatenate(spread, axis=0).astype(BF16)

    groups = [lax.rem(my_group + i, n_group) for i in range(1, n_group)]
    for k in range(chunks):
        columns = slice(k * chunk, (k + 1) * chunk)
        projected = base[:, columns] + lax.dot_general(
            spread, up_factors[:, columns], TN, preferred_element_type=F32
        )
        projected = projected.reshape(n_group, 2, rows, chunk).astype(BF16)
        for core in range(2):
            a1_out[k, core] = projected[:, core]
        send(
            a1_out.at[k, other_core], a1_in.at[k], chunk_send.at[0, k], chunk_recv.at[0, k],
            {"expert": partner},
        )
    for k in range(chunks):
        wait_bytes(a1_in.at[k], chunk_recv.at[0, k])
        a2_out[k] = (a1_out[k, my_core].astype(F32) + a1_in[k].astype(F32)).astype(BF16)
        for to in groups:
            send(
                a2_out.at[k, to], a2_in.at[k, my_group], chunk_send.at[1, k], chunk_recv.at[1, k],
                {"expert": to * 2 + my_core},
            )
        a2_in[k, my_group] = a2_out[k, my_group]
    attention = []
    for k in range(chunks):
        wait_bytes(a2_in.at[k, 0 : n_group - 1], chunk_recv.at[1, k])
        attention.append(jnp.sum(a2_in[k].astype(F32), axis=0))
    stream = residual[...].astype(F32) + jnp.concatenate(attention, axis=1)
    inverse_rms = lax.rsqrt(jnp.mean(stream * stream, axis=1, keepdims=True) + EPSILON)
    normed = stream * inverse_rms * gain[...].reshape(1, model_width).astype(F32)
    tok[my_core, my_dp, my_group] = normed.astype(BF16)

    def block(core, dp, group):
        return tok.at[core, dp, group], tok_sem.at[dp * n_group + group]

    own, own_sem = block(my_core, my_dp, my_group)
    for i in range(1, n_group):
        to = lax.rem(my_group + i, n_group) * 2 + my_core
        send(own, own, send_sem.at[4], own_sem, {"expert": to})
    for i in range(n_group):
        group = lax.rem(my_group + n_group - i, n_group)
        here, here_sem = block(my_core, my_dp, group)
        if i > 0:
            wait_bytes(here, here_sem)
        for j in range(1, n_dp):
            send(here, here, send_sem.at[5], here_sem, {"dp": lax.rem(my_dp + j, n_dp)})
        send(here, here, send_sem.at[6], recv_sem.at[4], {"expert": partner})
    for j in range(1, n_dp):
        from_dp = lax.rem(my_dp + n_dp - j, n_dp)
        for i in range(n_group):
            group = lax.rem(my_group + n_group - i, n_group)
            here, here_sem = block(my_core, from_dp, group)
            wait_bytes(here, here_sem)
            send(here, here, send_sem.at[6], recv_sem.at[4], {"expert": partner})

    all_rows = 2 * n_dp * n_group * rows
    wait_bytes(dense_gates.at[0 : n_expert - 1], recv_sem.at[3])
    weight = []
    for core in range(2):
        for dp in range(n_dp):
            of_rows = dense_gates[
                pl.ds(core, n_group, stride=2), dp * rows : (dp + 1) * rows, :
            ].reshape(n_group * rows, LANES)
            lanes = lax.broadcasted_iota(jnp.int32, of_rows.shape, 1)
            weight.append(jnp.sum(jnp.where(lanes == me, of_rows, 0.0), axis=1, keepdims=True))
    weight = jnp.concatenate(weight, axis=0)
    for k in (8, 9, 10):
        small[k].wait()
    wait_bytes(tok.at[0], recv_sem.at[4])
    tokens = tok[...].reshape(all_rows, model_width)
    gate_act = jnp.dot(tokens, w_gate[0], preferred_element_type=F32)
    up_act = jnp.dot(tokens, w_up[0], preferred_element_type=F32)
    hidden = (gate_act / (1.0 + jnp.exp(-gate_act)) * up_act).astype(BF16)

    for k in range(chunks):
        made = lax.dot_general(
            hidden, w_down[0, k * chunk : (k + 1) * chunk, :], NT, preferred_element_type=F32
        )
        r1_out[k] = (made * weight).reshape(2, n_dp, n_group, rows, chunk).astype(BF16)
        send(
            r1_out.at[k, other_core], r1_in.at[k], chunk_send.at[2, k], chunk_recv.at[2, k],
            {"expert": partner},
        )
    for k in range(chunks):
        wait_bytes(r1_in.at[k], chunk_recv.at[2, k])
        r2_out[k] = (r1_out[k, my_core].astype(F32) + r1_in[k].astype(F32)).astype(BF16)
        for j in range(1, n_dp):
            to = lax.rem(my_dp + j, n_dp)
            send(
                r2_out.at[k, to], r2_in.at[k, my_dp], chunk_send.at[3, k], chunk_recv.at[3, k],
                {"dp": to},
            )
        r2_in[k, my_dp] = r2_out[k, my_dp]
    for k in range(chunks):
        if n_dp > 1:
            wait_bytes(r2_in.at[k, 0 : n_dp - 1], chunk_recv.at[3, k])
        r3_out[k] = jnp.sum(r2_in[k].astype(F32), axis=0).astype(BF16)
        for to in groups:
            send(
                r3_out.at[k, to], r3_in.at[k, my_group], chunk_send.at[4, k], chunk_recv.at[4, k],
                {"expert": to * 2 + my_core},
            )
        r3_in[k, my_group] = r3_out[k, my_group]
    for k in range(chunks):
        wait_bytes(r3_in.at[k, 0 : n_group - 1], chunk_recv.at[4, k])
        routed = jnp.sum(r3_in[k].astype(F32), axis=0)
        columns = slice(k * chunk, (k + 1) * chunk)
        out_ref[:, columns] = (stream[:, columns] + routed).astype(BF16)

    for k, ref in enumerate((att, names, lora, dense_gates)):
        wait_bytes(ref.at[0 : n_expert - 1], send_sem.at[k])
    wait_bytes(tok.at[0, 0, 0 : n_group - 1], send_sem.at[4])
    if n_dp > 1:
        wait_bytes(tok.at[0, 0 : n_dp - 1], send_sem.at[5])
    wait_bytes(tok.at[0], send_sem.at[6])
    for k in range(chunks):
        wait_bytes(a1_in.at[k], chunk_send.at[0, k])
        wait_bytes(a2_out.at[k, 0 : n_group - 1], chunk_send.at[1, k])
        wait_bytes(r1_in.at[k], chunk_send.at[2, k])
        if n_dp > 1:
            wait_bytes(r2_out.at[k, 0 : n_dp - 1], chunk_send.at[3, k])
        wait_bytes(r3_out.at[k, 0 : n_group - 1], chunk_send.at[4, k])


def local(
    n_expert,
    n_dp,
    q_latent,
    latent_cache,
    lengths,
    residual,
    adapter_ids,
    value_out,
    adapter_down,
    adapter_up_factors,
    norm_gain,
    expert_ids,
    gate_weights,
    w_gate,
    w_up,
    w_down,
):
    rows, model_width = residual.shape
    column, top = expert_ids.shape
    heads = q_latent.shape[1]
    width = heads * LAT // n_expert
    n_group = n_expert // 2
    packed = 2 if n_expert * rows * 2 == LANES else 1
    lane_rows = packed * n_expert * rows
    chunks = CHUNKS
    chunk = model_width // chunks
    big = (
        q_latent,
        latent_cache.swapaxes(1, 2),
        residual,
        value_out,
        adapter_down,
        adapter_up_factors,
        norm_gain,
        expert_ids,
        gate_weights,
        w_gate,
        w_up,
        w_down,
    )
    any_spec = pl.BlockSpec(memory_space=pl.ANY)
    smem_spec = pl.BlockSpec(memory_space=pltpu.SMEM)
    dma = pltpu.SemaphoreType.DMA
    to_groups = (n_group, rows, chunk)
    to_all = (n_dp,) + to_groups
    return pl.pallas_call(
        functools.partial(layer_kernel, (n_expert, n_dp, top)),
        out_shape=jax.ShapeDtypeStruct((rows, model_width), BF16),
        in_specs=[smem_spec] * 2 + [any_spec] * len(big),
        out_specs=pl.BlockSpec(memory_space=pltpu.VMEM),
        scratch_shapes=[pltpu.VMEM(a.shape, a.dtype) for a in big]
        + [
            pltpu.VMEM((n_expert, rows, LANES), F32),
            pltpu.VMEM((n_expert, column, LANES), F32),
            pltpu.VMEM((n_expert, rows, width), BF16),
            pltpu.VMEM((n_expert, rows, width), BF16),
            pltpu.VMEM((n_expert, ADAPTER_RANK // packed, lane_rows), F32),
            pltpu.VMEM((chunks, 2) + to_groups, BF16),
            pltpu.VMEM((chunks,) + to_groups, BF16),
            pltpu.VMEM((chunks,) + to_groups, BF16),
            pltpu.VMEM((chunks,) + to_groups, BF16),
            pltpu.VMEM((2, n_dp, n_group, rows, model_width), BF16),
            pltpu.VMEM((chunks, 2) + to_all, BF16),
            pltpu.VMEM((chunks,) + to_all, BF16),
            pltpu.VMEM((chunks,) + to_all, BF16),
            pltpu.VMEM((chunks,) + to_all, BF16),
            pltpu.VMEM((chunks,) + to_groups, BF16),
            pltpu.VMEM((chunks,) + to_groups, BF16),
            dma((rows,)),
            dma((11,)),
            dma((10,)),
            dma((8,)),
            dma((n_dp * n_group,)),
            dma((5, chunks)),
            dma((5, chunks)),
        ],
        compiler_params=pltpu.CompilerParams(
            collective_id=0, has_side_effects=True, vmem_limit_bytes=64000000
        ),
        name="layer",
    )(lengths, adapter_ids, *big)


def solution(mesh):
    in_specs = (
        P(("expert", "dp"), None, None),
        P(("expert", "dp"), None, None),
        P(("expert", "dp")),
        P(("expert", "dp"), None),
        P(("expert", "dp")),
        P("expert", None),
        P("expert", None),
        P("expert", None),
        P(),
        P("expert", None),
        P("expert", None),
        P("expert", None, "dp"),
        P("expert", None, "dp"),
        P("expert", None, "dp"),
    )
    return jax.shard_map(
        functools.partial(local, mesh.shape["expert"], mesh.shape["dp"]),
        mesh=mesh,
        in_specs=in_specs,
        out_specs=P(("expert", "dp"), None),
        check_vma=False,
    )
```

```python
import functools

import jax
import jax.numpy as jnp
from jax import lax
from jax.experimental import pallas as pl
from jax.experimental.pallas import tpu as pltpu
from jax.sharding import PartitionSpec as P

LAT = 512
ADAPTER_RANK = 16
SOFTMAX_SCALE = 192.0 ** (-0.5)
ADAPTER_SCALE = 2.0
EPSILON = 1e-06
LANES = 128
CHUNKS = 4
MESH = pl.DeviceIdType.MESH
F32 = jnp.float32
BF16 = jnp.bfloat16
NT = (((1,), (1,)), ((), ()))
TN = (((0,), (0,)), ((), ()))


def layer_kernel(
    dims,
    lengths,
    adapter_ids,
    q_hbm,
    cache_hbm,
    residual_hbm,
    value_hbm,
    down_hbm,
    upf_hbm,
    gain_hbm,
    ids_hbm,
    gates_hbm,
    wg_hbm,
    wu_hbm,
    wd_hbm,
    out_ref,
    q,
    cache,
    residual,
    value_out,
    adapter_down,
    up_factors,
    gain,
    ids,
    gates,
    w_gate,
    w_up,
    w_down,
    names,
    dense_gates,
    att,
    pieces,
    lora,
    a1_out,
    a1_in,
    a2_out,
    a2_in,
    tok,
    r1_out,
    r1_in,
    r2_out,
    r2_in,
    r3_out,
    r3_in,
    cache_sem,
    load_sem,
    send_sem,
    recv_sem,
    tok_sem,
    chunk_send,
    chunk_recv,
):
    n_expert, n_dp, top = dims
    n_group = n_expert // 2
    me = lax.axis_index("expert")
    my_dp = lax.axis_index("dp")
    my_group = me // 2
    my_core = lax.rem(me, 2)
    other_core = 1 - my_core
    partner = my_group * 2 + other_core
    far_first = sorted(range(1, n_group), key=lambda i: -min(i, n_group - i))
    rows, model_width = residual.shape
    column = ids.shape[0]
    heads = q.shape[1]
    width = att.shape[2]
    group_rows = n_expert * rows
    chunks = a1_out.shape[0]
    chunk = model_width // chunks
    packed = ADAPTER_RANK // lora.shape[1]

    cache_loads = []
    for r in range(rows):
        cache_loads.append(pltpu.make_async_copy(cache_hbm.at[r], cache.at[r], cache_sem.at[r]))
    small = []
    for k, (src, dst) in enumerate(
        (
            (q_hbm, q),
            (ids_hbm, ids),
            (gates_hbm, gates),
            (residual_hbm, residual),
            (gain_hbm, gain),
            (down_hbm, adapter_down),
            (value_hbm, value_out),
            (upf_hbm, up_factors),
            (wg_hbm, w_gate),
            (wu_hbm, w_up),
            (wd_hbm, w_down),
        )
    ):
        small.append(pltpu.make_async_copy(src, dst, load_sem.at[k]))
    small[0].start()
    for load in cache_loads:
        load.start()

    barrier = pltpu.get_barrier_semaphore()
    for i in range(1, n_expert):
        pl.semaphore_signal(
            barrier, inc=1, device_id={"expert": lax.rem(me + i, n_expert)}, device_id_type=MESH
        )
    for i in range(1, n_dp):
        pl.semaphore_signal(
            barrier, inc=1, device_id={"dp": lax.rem(my_dp + i, n_dp)}, device_id_type=MESH
        )

    def send(src, dst, sends, recvs, where):
        pltpu.make_async_remote_copy(
            src_ref=src, dst_ref=dst, send_sem=sends, recv_sem=recvs, device_id=where,
            device_id_type=MESH,
        ).start()

    def wait_bytes(ref, sem):
        pltpu.make_async_copy(ref, ref, sem).wait()

    small[0].wait()
    for load in cache_loads:
        load.wait()
    for k in (5, 6, 7, 1, 2, 3, 4, 8, 9, 10):
        small[k].start()
    all_scores = []
    for r in range(rows):
        scores = jnp.dot(q[r], cache[r], preferred_element_type=F32) * SOFTMAX_SCALE
        position = lax.broadcasted_iota(jnp.int32, scores.shape, 1)
        all_scores.append(jnp.where(position < lengths[r], scores, -1e30))
    all_scores = jnp.concatenate(all_scores, axis=0)
    raised = jnp.exp(all_scores - jnp.max(all_scores, axis=1, keepdims=True))
    weights = (raised / jnp.sum(raised, axis=1, keepdims=True)).astype(BF16)

    row_of = lax.broadcasted_iota(jnp.int32, (rows, LANES), 0)
    named = jnp.zeros((rows, LANES), jnp.int32)
    for r in range(rows):
        named = jnp.where(row_of == r, adapter_ids[r], named)
    names[me] = named.astype(F32)
    peers = [lax.rem(me + i, n_expert) for i in range(1, n_expert)]
    pl.semaphore_wait(barrier, n_expert - 1 + n_dp - 1)
    for to in peers:
        send(names.at[me], names.at[me], send_sem.at[1], recv_sem.at[1], {"expert": to})
    outs = []
    for r in range(rows):
        of_request = weights[r * heads : (r + 1) * heads]
        outs.append(
            lax.dot_general(of_request, cache[r, :LAT], NT, preferred_element_type=F32)
        )
    by_head = jnp.stack(outs, axis=1).astype(BF16)
    parts = LAT // width
    if parts == 1:
        att[...] = by_head
    else:
        for h in range(heads):
            for part in range(parts):
                att[h * parts + part] = by_head[h, :, part * width : (part + 1) * width]

    for to in peers:
        send(att.at[to], pieces.at[me], send_sem.at[0], recv_sem.at[0], {"expert": to})
    pieces[me] = att[me]

    small[5].wait()
    fold_shape = (ADAPTER_RANK, adapter_down.shape[1])
    fold = (
        lax.rem(lax.broadcasted_iota(jnp.int32, fold_shape, 1), ADAPTER_RANK)
        == lax.broadcasted_iota(jnp.int32, fold_shape, 0)
    ).astype(F32).astype(BF16)
    wait_bytes(pieces.at[0 : n_expert - 1], recv_sem.at[0])
    latent = pieces[...].reshape(group_rows, width)
    full = jnp.dot(latent, adapter_down[...], preferred_element_type=F32)
    of_column = lax.broadcasted_iota(jnp.int32, full.shape, 1) // ADAPTER_RANK
    wait_bytes(names.at[0 : n_expert - 1], recv_sem.at[1])
    adapter_of = names[...].reshape(group_rows, LANES)
    chosen = jnp.where(of_column.astype(F32) == adapter_of[:, 0:1], full, 0.0)
    high = chosen.astype(BF16)
    low = (chosen - high.astype(F32)).astype(BF16)
    down_part = lax.dot_general(fold, high, NT, preferred_element_type=F32) + lax.dot_general(
        fold, low, NT, preferred_element_type=F32
    )
    if packed == 2:
        half = ADAPTER_RANK // 2
        down_part = jnp.concatenate([down_part[:half], down_part[half:]], axis=1)
    lora[me] = down_part
    for to in peers:
        send(lora.at[me], lora.at[me], send_sem.at[2], recv_sem.at[2], {"expert": to})

    small[1].wait()
    small[2].wait()
    lane = lax.broadcasted_iota(jnp.int32, (column, LANES), 1)
    dense = jnp.zeros((column, LANES), F32)
    for k in range(top):
        dense += jnp.where(lane == ids[:, k : k + 1], gates[:, k : k + 1], 0.0)
    dense_gates[me] = dense
    for to in peers:
        mine = dense_gates.at[me]
        send(mine, mine, send_sem.at[3], recv_sem.at[3], {"expert": to})

    small[6].wait()
    base = jnp.dot(latent, value_out[...], preferred_element_type=F32)
    small[7].wait()
    small[3].wait()
    small[4].wait()
    pad_rows = -group_rows % LANES
    if pad_rows:
        adapter_of = jnp.concatenate([adapter_of, jnp.zeros((pad_rows, LANES), F32)], axis=0)
    adapter_lane = adapter_of.T[0:1, :group_rows]
    wait_bytes(lora.at[0 : n_expert - 1], recv_sem.at[2])
    scaled = (ADAPTER_SCALE * jnp.sum(lora[...], axis=0)).astype(BF16).astype(F32)
    if packed == 2:
        scaled = jnp.concatenate([scaled[:, :group_rows], scaled[:, group_rows:]], axis=0)
    owned = up_factors.shape[0] // ADAPTER_RANK
    spread = []
    for o in range(owned):
        holds = adapter_lane == (me * owned + o).astype(F32)
        spread.append(jnp.where(holds, scaled, 0.0))
    spread = jnp.concatenate(spread, axis=0).astype(BF16)

    groups = [lax.rem(my_group + i, n_group) for i in far_first]
    for k in range(chunks):
        columns = slice(k * chunk, (k + 1) * chunk)
        projected = base[:, columns] + lax.dot_general(
            spread, up_factors[:, columns], TN, preferred_element_type=F32
        )
        projected = projected.reshape(n_group, 2, rows, chunk).astype(BF16)
        for core in range(2):
            a1_out[k, core] = projected[:, core]
        send(
            a1_out.at[k, other_core], a1_in.at[k], chunk_send.at[0, k], chunk_recv.at[0, k],
            {"expert": partner},
        )
    for k in range(chunks):
        wait_bytes(a1_in.at[k], chunk_recv.at[0, k])
        a2_out[k] = (a1_out[k, my_core].astype(F32) + a1_in[k].astype(F32)).astype(BF16)
        for to in groups:
            send(
                a2_out.at[k, to], a2_in.at[k, my_group], chunk_send.at[1, k], chunk_recv.at[1, k],
                {"expert": to * 2 + my_core},
            )
        a2_in[k, my_group] = a2_out[k, my_group]
    attention = []
    for k in range(chunks):
        wait_bytes(a2_in.at[k, 0 : n_group - 1], chunk_recv.at[1, k])
        attention.append(jnp.sum(a2_in[k].astype(F32), axis=0))
    stream = residual[...].astype(F32) + jnp.concatenate(attention, axis=1)
    inverse_rms = lax.rsqrt(jnp.mean(stream * stream, axis=1, keepdims=True) + EPSILON)
    normed = stream * inverse_rms * gain[...].reshape(1, model_width).astype(F32)
    tok[my_core, my_dp, my_group] = normed.astype(BF16)

    def block(core, dp, group):
        return tok.at[core, dp, group], tok_sem.at[dp * n_group + group]

    own, own_sem = block(my_core, my_dp, my_group)
    for i in far_first:
        to = lax.rem(my_group + i, n_group) * 2 + my_core
        send(own, own, send_sem.at[4], own_sem, {"expert": to})
    for i in range(n_group):
        group = lax.rem(my_group + n_group - i, n_group)
        here, here_sem = block(my_core, my_dp, group)
        if i > 0:
            wait_bytes(here, here_sem)
        for j in range(1, n_dp):
            send(here, here, send_sem.at[5], here_sem, {"dp": lax.rem(my_dp + j, n_dp)})
        send(here, here, send_sem.at[6], recv_sem.at[4], {"expert": partner})
    for j in range(1, n_dp):
        from_dp = lax.rem(my_dp + n_dp - j, n_dp)
        for i in range(n_group):
            group = lax.rem(my_group + n_group - i, n_group)
            here, here_sem = block(my_core, from_dp, group)
            wait_bytes(here, here_sem)
            send(here, here, send_sem.at[6], recv_sem.at[4], {"expert": partner})

    all_rows = 2 * n_dp * n_group * rows
    wait_bytes(dense_gates.at[0 : n_expert - 1], recv_sem.at[3])
    weight = []
    for core in range(2):
        for dp in range(n_dp):
            of_rows = dense_gates[
                pl.ds(core, n_group, stride=2), dp * rows : (dp + 1) * rows, :
            ].reshape(n_group * rows, LANES)
            lanes = lax.broadcasted_iota(jnp.int32, of_rows.shape, 1)
            weight.append(jnp.sum(jnp.where(lanes == me, of_rows, 0.0), axis=1, keepdims=True))
    weight = jnp.concatenate(weight, axis=0)
    for k in (8, 9, 10):
        small[k].wait()
    wait_bytes(tok.at[0], recv_sem.at[4])
    tokens = tok[...].reshape(all_rows, model_width)
    gate_act = jnp.dot(tokens, w_gate[0], preferred_element_type=F32)
    up_act = jnp.dot(tokens, w_up[0], preferred_element_type=F32)
    hidden = (gate_act / (1.0 + jnp.exp(-gate_act)) * up_act).astype(BF16)

    for k in range(chunks):
        made = lax.dot_general(
            hidden, w_down[0, k * chunk : (k + 1) * chunk, :], NT, preferred_element_type=F32
        )
        r1_out[k] = (made * weight).reshape(2, n_dp, n_group, rows, chunk).astype(BF16)
        send(
            r1_out.at[k, other_core], r1_in.at[k], chunk_send.at[2, k], chunk_recv.at[2, k],
            {"expert": partner},
        )
    for k in range(chunks):
        wait_bytes(r1_in.at[k], chunk_recv.at[2, k])
        r2_out[k] = (r1_out[k, my_core].astype(F32) + r1_in[k].astype(F32)).astype(BF16)
        for j in range(1, n_dp):
            to = lax.rem(my_dp + j, n_dp)
            send(
                r2_out.at[k, to], r2_in.at[k, my_dp], chunk_send.at[3, k], chunk_recv.at[3, k],
                {"dp": to},
            )
        r2_in[k, my_dp] = r2_out[k, my_dp]
    for k in range(chunks):
        if n_dp > 1:
            wait_bytes(r2_in.at[k, 0 : n_dp - 1], chunk_recv.at[3, k])
        r3_out[k] = jnp.sum(r2_in[k].astype(F32), axis=0).astype(BF16)
        for to in groups:
            send(
                r3_out.at[k, to], r3_in.at[k, my_group], chunk_send.at[4, k], chunk_recv.at[4, k],
                {"expert": to * 2 + my_core},
            )
        r3_in[k, my_group] = r3_out[k, my_group]
    for k in range(chunks):
        wait_bytes(r3_in.at[k, 0 : n_group - 1], chunk_recv.at[4, k])
        routed = jnp.sum(r3_in[k].astype(F32), axis=0)
        columns = slice(k * chunk, (k + 1) * chunk)
        out_ref[:, columns] = (stream[:, columns] + routed).astype(BF16)

    for k, ref in enumerate((att, names, lora, dense_gates)):
        wait_bytes(ref.at[0 : n_expert - 1], send_sem.at[k])
    wait_bytes(tok.at[0, 0, 0 : n_group - 1], send_sem.at[4])
    if n_dp > 1:
        wait_bytes(tok.at[0, 0 : n_dp - 1], send_sem.at[5])
    wait_bytes(tok.at[0], send_sem.at[6])
    for k in range(chunks):
        wait_bytes(a1_in.at[k], chunk_send.at[0, k])
        wait_bytes(a2_out.at[k, 0 : n_group - 1], chunk_send.at[1, k])
        wait_bytes(r1_in.at[k], chunk_send.at[2, k])
        if n_dp > 1:
            wait_bytes(r2_out.at[k, 0 : n_dp - 1], chunk_send.at[3, k])
        wait_bytes(r3_out.at[k, 0 : n_group - 1], chunk_send.at[4, k])


def local(
    n_expert,
    n_dp,
    q_latent,
    latent_cache,
    lengths,
    residual,
    adapter_ids,
    value_out,
    adapter_down,
    adapter_up_factors,
    norm_gain,
    expert_ids,
    gate_weights,
    w_gate,
    w_up,
    w_down,
):
    rows, model_width = residual.shape
    column, top = expert_ids.shape
    heads = q_latent.shape[1]
    width = heads * LAT // n_expert
    n_group = n_expert // 2
    packed = 2 if n_expert * rows * 2 == LANES else 1
    lane_rows = packed * n_expert * rows
    chunks = CHUNKS
    chunk = model_width // chunks
    big = (
        q_latent,
        latent_cache.swapaxes(1, 2),
        residual,
        value_out,
        adapter_down,
        adapter_up_factors,
        norm_gain,
        expert_ids,
        gate_weights,
        w_gate,
        w_up,
        w_down,
    )
    any_spec = pl.BlockSpec(memory_space=pl.ANY)
    smem_spec = pl.BlockSpec(memory_space=pltpu.SMEM)
    dma = pltpu.SemaphoreType.DMA
    to_groups = (n_group, rows, chunk)
    to_all = (n_dp,) + to_groups
    return pl.pallas_call(
        functools.partial(layer_kernel, (n_expert, n_dp, top)),
        out_shape=jax.ShapeDtypeStruct((rows, model_width), BF16),
        in_specs=[smem_spec] * 2 + [any_spec] * len(big),
        out_specs=pl.BlockSpec(memory_space=pltpu.VMEM),
        scratch_shapes=[pltpu.VMEM(a.shape, a.dtype) for a in big]
        + [
            pltpu.VMEM((n_expert, rows, LANES), F32),
            pltpu.VMEM((n_expert, column, LANES), F32),
            pltpu.VMEM((n_expert, rows, width), BF16),
            pltpu.VMEM((n_expert, rows, width), BF16),
            pltpu.VMEM((n_expert, ADAPTER_RANK // packed, lane_rows), F32),
            pltpu.VMEM((chunks, 2) + to_groups, BF16),
            pltpu.VMEM((chunks,) + to_groups, BF16),
            pltpu.VMEM((chunks,) + to_groups, BF16),
            pltpu.VMEM((chunks,) + to_groups, BF16),
            pltpu.VMEM((2, n_dp, n_group, rows, model_width), BF16),
            pltpu.VMEM((chunks, 2) + to_all, BF16),
            pltpu.VMEM((chunks,) + to_all, BF16),
            pltpu.VMEM((chunks,) + to_all, BF16),
            pltpu.VMEM((chunks,) + to_all, BF16),
            pltpu.VMEM((chunks,) + to_groups, BF16),
            pltpu.VMEM((chunks,) + to_groups, BF16),
            dma((rows,)),
            dma((11,)),
            dma((10,)),
            dma((8,)),
            dma((n_dp * n_group,)),
            dma((5, chunks)),
            dma((5, chunks)),
        ],
        compiler_params=pltpu.CompilerParams(
            collective_id=0, has_side_effects=True, vmem_limit_bytes=64000000
        ),
        name="layer",
    )(lengths, adapter_ids, *big)


def solution(mesh):
    in_specs = (
        P(("expert", "dp"), None, None),
        P(("expert", "dp"), None, None),
        P(("expert", "dp")),
        P(("expert", "dp"), None),
        P(("expert", "dp")),
        P("expert", None),
        P("expert", None),
        P("expert", None),
        P(),
        P("expert", None),
        P("expert", None),
        P("expert", None, "dp"),
        P("expert", None, "dp"),
        P("expert", None, "dp"),
    )
    return jax.shard_map(
        functools.partial(local, mesh.shape["expert"], mesh.shape["dp"]),
        mesh=mesh,
        in_specs=in_specs,
        out_specs=P(("expert", "dp"), None),
        check_vma=False,
    )
```
